128 devices in a mesh: row: 16 (over y, x_lo, core), col: 8 (over z, x_hi).
Axes of the slice: x: 4 (x_hi: 2, x_lo: 2; x = x_hi * 2 + x_lo), y: 4, z: 4, core: 2. Of those that a mesh axis runs over, the one named last changes fastest.
Arguments:
- tokens: bfloat16 [2048, 16384], P('col', 'row'), may hold values from -160 to 160
- norm_gain: bfloat16 [16384], P('row'), may hold values from 0.5 to 1.5
- gate_weight: bfloat16 [16384, 26624], P('row', 'col'), may hold values from -0.046875 to 0.046875
Outputs:
- gate_out: float32 [2048, 26624], P('row', 'col')
- token_peak: float32 [2048], P('col')
The draws below stay inside these ranges and needn't reach their ends.
All inputs are finite; a program needn't handle non-finite values.
Results may differ from the reference program's by a relative error of at most 0.008.
Values may be sent and summed in bfloat16 or wider, within the bound.
No kernel may reach another device: no remote copies, remote signals or barrier semaphores. Data moves between devices by JAX's collectives and lax.ppermute only.
A program may use at most 128 MiB of HBM per device.

```python
import math
import jax
import jax.numpy as jnp
from jax import lax

D = 16384
FFW = 26624
TOKENS = 2048


def draw_tokens(key, part):
    key_base, key_rough, key_rows = jax.random.split(key, 3)
    place = jnp.arange(D, dtype=jnp.float32) / (D - 1)
    rising = 0.6 + 1.2 * place
    rough = jax.random.uniform(key_rough, (D,), jnp.float32, 0.7, 1.4)
    row_scale = jnp.exp(jax.random.uniform(key_rows, (TOKENS, 1), jnp.float32, 0.0, math.log(10.0)))
    base = jnp.clip(jax.random.normal(key_base, (TOKENS, D), jnp.float32), -6.0, 6.0)
    values = base * (rising * rough)[None, :] * row_scale
    return jnp.clip(values, -160.0, 160.0).astype(jnp.bfloat16)


def block_scale(rng, dims, shards, least, top_value):
    loudness = 1.0
    for position, shards_of in shards:
        heights = jax.random.uniform(jax.random.fold_in(jax.random.fold_in(rng, 6), position), (shards_of,), jnp.float32, least / len(shards), top_value / len(shards))
        loudness = loudness * jnp.repeat(jnp.exp(heights), dims[position] // shards_of).reshape((-1,) + (1,) * (len(dims) - 1 - position))
    return loudness


def noise(stream_key, dims, scale, limit, pieces=(), kind=jnp.bfloat16):
    result = scale * jax.random.normal(stream_key, dims, jnp.float32)
    if pieces:
        result = result * block_scale(stream_key, dims, pieces, -0.22, 0.18)
    return jnp.clip(result, -limit, limit).astype(kind)


def setup_inputs(seed: int = 0) -> dict:
    streams_of = jax.random.split(jax.random.key(seed), 4)
    tokens = draw_tokens(jax.random.fold_in(streams_of[3], 71), 0)
    norm_gain = jnp.clip(1.0 + 0.1 * jax.random.normal(streams_of[1], (D,), jnp.float32), 0.5, 1.5).astype(jnp.bfloat16)
    gate_weight = noise(streams_of[2], (D, FFW), D ** -0.5, 0.046875, ((0, 16), (1, 8)))
    return dict(tokens=tokens, norm_gain=norm_gain, gate_weight=gate_weight)


def reference(tokens, norm_gain, gate_weight):
    values = tokens.astype(jnp.float32)
    mean_square = lax.optimization_barrier(jnp.sum(values * values, axis=1)) / D
    inverse = lax.rsqrt(mean_square + 1e-05)
    normed = values * inverse[:, None] * norm_gain.astype(jnp.float32)[None, :]
    token_peak = lax.optimization_barrier(jnp.max(jnp.abs(normed), axis=1))
    scale = ((token_peak + 1e-06) / 448.0).astype(jnp.bfloat16)
    quant = (normed / scale.astype(jnp.float32)[:, None]).astype(jnp.bfloat16)
    product = jnp.dot(quant, gate_weight, preferred_element_type=jnp.float32)
    gate_out = product * scale.astype(jnp.float32)[:, None]
    return (gate_out, token_peak)
```

```python
import functools
import jax
import jax.numpy as jnp
from jax import lax
from jax.experimental import pallas as pl
from jax.experimental.pallas import tpu as pltpu
from jax.sharding import PartitionSpec as P

D = 16384
AXES = ("row", "col")
CHUNKS = ((0, 128),)
ORDER = (7, 6, 5, 3, 4, 2, 1, 0)
TILE = 256


def place(y, xl, core, z, xh):
    return (y * 4 + xl * 2 + core) * 8 + z * 2 + xh


def pairs(move):
    out = []
    for y in range(4):
        for xl in range(2):
            for core in range(2):
                for z in range(4):
                    for xh in range(2):
                        out.append((place(y, xl, core, z, xh), place(*move(y, xl, core, z, xh))))
    return out


MOVES = {
    "core": pairs(lambda y, xl, core, z, xh: (y, xl, 1 - core, z, xh)),
    "ya": pairs(lambda y, xl, core, z, xh: (y ^ 1, xl, core, z, xh)),
    "yb": pairs(lambda y, xl, core, z, xh: (3 - y, xl, core, z, xh)),
    "xl": pairs(lambda y, xl, core, z, xh: (y, 1 - xl, core, z, xh)),
    "za": pairs(lambda y, xl, core, z, xh: (y, xl, core, z ^ 1, xh)),
    "zb": pairs(lambda y, xl, core, z, xh: (y, xl, core, 3 - z, xh)),
    "xh": pairs(lambda y, xl, core, z, xh: (y, xl, core, z, 1 - xh)),
    "turn": pairs(lambda y, xl, core, z, xh: (z, xh, core, y, xl)),
}


def send(array, move):
    return lax.ppermute(array, AXES, MOVES[move])


def thirds(rows):
    unit = rows // 16
    first = -(-unit // 3)
    second = -(-(unit - first) // 2)
    cuts = (0, first * 16, (first + second) * 16, rows)
    return tuple(zip(cuts[:-1], cuts[1:]))


def gathered(block):
    parts = thirds(block.shape[1])
    a, b, x = send(block, "za"), send(block, "zb"), send(block, "xh")
    ax, ab, bx = send(x, "za"), send(a, "zb"), send(b, "xh")
    last = [
        send(lax.slice_in_dim(source, *part, axis=1), move)
        for source, part, move in zip((bx, ax, ab), parts, ("za", "zb", "xh"))
    ]
    return [block, x, b, bx, a, ax, ab], last


def multiply(rows, parts, first, group):
    count = 4 * rows
    base = 0 if first else count

    def kernel(slot, *refs):
        blocks, refs = refs[:7], refs[7:]
        last, refs = refs[: len(parts)], refs[len(parts) :]
        near, far, refs = refs[0], refs[1], refs[2:]
        outs, (held, sems) = refs[:-2], refs[-2:]

        @pl.when(pl.program_id(0) == 0)
        def _():
            copies = []
            for k in range(7):
                where = pl.ds(pl.multiple_of(slot[k] * rows, rows), rows)
                copies.append(pltpu.make_async_copy(blocks[k], held.at[:, where, :], sems.at[k]))
            for n, (low, high) in enumerate(parts):
                where = pl.ds(pl.multiple_of(slot[7] * rows + low, 16), high - low)
                copies.append(pltpu.make_async_copy(last[n], held.at[:, where, :], sems.at[7 + n]))
            for copy in copies:
                copy.start()
            for copy in copies:
                copy.wait()

        got = jnp.dot(held[0, base : base + count, :], near[...], preferred_element_type=jnp.float32)
        got += jnp.dot(held[1, base : base + count, :], far[...], preferred_element_type=jnp.float32)
        at = 0
        for out in outs:
            out[...] = got[at : at + out.shape[0], :].astype(out.dtype)
            at += out.shape[0]

    width = 3328
    if first:
        kinds = [(high - low, jnp.bfloat16) for low, high in parts] + [(rows, jnp.float32)] * 3
    else:
        kinds = [(rows, jnp.float32)] * 4
    anywhere = pl.BlockSpec(memory_space=pl.ANY)
    slab = pl.BlockSpec((1024, TILE), lambda j, slot: (0, j))
    return pl.pallas_call(
        kernel,
        grid_spec=pltpu.PrefetchScalarGridSpec(
            num_scalar_prefetch=1,
            grid=(width // TILE,),
            in_specs=[anywhere] * (7 + len(parts)) + [slab, slab],
            out_specs=[pl.BlockSpec((n, TILE), lambda j, slot: (0, j)) for n, _ in kinds],
            scratch_shapes=[
                pltpu.VMEM((2, 8 * rows, 1024), jnp.bfloat16),
                pltpu.SemaphoreType.DMA((7 + len(parts),)),
            ],
        ),
        out_shape=[jax.ShapeDtypeStruct((n, width), kind) for n, kind in kinds],
        compiler_params=pltpu.CompilerParams(vmem_limit_bytes=24 << 20),
        cost_estimate=pl.CostEstimate(
            flops=2 * count * 2048 * width, bytes_accessed=14 << 20, transcendentals=0
        ),
        name=f"multiply_{group}",
    )


def grown(total, part, low):
    rows = total.shape[0]
    wide = jnp.pad(part.astype(jnp.float32), ((low, rows - low - part.shape[0]), (0, 0)))
    return (total + wide).astype(jnp.bfloat16)


def plus(total, part):
    return (total + part.astype(jnp.float32)).astype(jnp.bfloat16)


def shards(tokens, norm_gain, gate_weight):
    row, col = lax.axis_index("row"), lax.axis_index("col")
    core = row % 2
    y, xl, z, xh = row // 4, (row // 2) % 2, col // 2, col % 2

    def bits(ring, x):
        return (((ring + 1) // 2) % 2) * 4 + (ring // 2) * 2 + x

    apart = bits(y, xl) ^ bits(z, xh)
    order = jnp.array([ORDER.index(k) for k in range(8)], jnp.int32)
    slots = order[jnp.arange(8, dtype=jnp.int32) ^ apart]

    far_weight = send(gate_weight, "core")
    values = tokens.astype(jnp.float32)
    gain = norm_gain.astype(jnp.float32)[None, :]
    weighted = values * gain
    squares = jnp.sum(values * values, axis=1)
    peak = jnp.max(jnp.abs(weighted), axis=1)
    lifted = weighted.astype(jnp.bfloat16).reshape(2, 128, 1024)
    mine = lax.dynamic_index_in_dim(lifted, core, 0)
    theirs = lax.dynamic_index_in_dim(lifted, 1 - core, 0)
    both = jnp.concatenate([mine, send(theirs, "core")], axis=0)

    stats = jnp.stack([squares, peak])
    for move in ("core", "ya", "yb", "xl"):
        other = send(stats, move)
        stats = jnp.stack([stats[0] + other[0], jnp.maximum(stats[1], other[1])])
    inverse = lax.rsqrt(stats[0] / D + 1e-05)
    token_peak = stats[1] * inverse
    scale = ((token_peak + 1e-06) / 448.0).astype(jnp.bfloat16).astype(jnp.float32)
    factors = jnp.stack([inverse / scale, scale]).reshape(2, 2, 128)
    factors = send(lax.dynamic_index_in_dim(factors, core, 1, keepdims=False), "turn")

    outs = []
    for number, (low, high) in enumerate(CHUNKS):
        rows = high - low
        parts = thirds(rows)
        blocks, last = gathered(both[:, low:high, :])
        feed = (slots, *blocks, *last, gate_weight, far_weight)
        *corner, ab, ax, bx = multiply(rows, parts, True, 2 * number)(*feed)
        a, b, x, own = multiply(rows, parts, False, 2 * number + 1)(*feed)
        to_bx, to_ax, to_ab = (send(p, m) for p, m in zip(corner, ("ya", "yb", "xl")))
        to_b = send(grown(bx, to_bx, parts[0][0]), "xl")
        to_x = send(grown(ax, to_ax, parts[1][0]), "ya")
        to_a = send(grown(ab, to_ab, parts[2][0]), "yb")
        ends = [send(plus(a, to_a), "ya"), send(plus(b, to_b), "yb"), send(plus(x, to_x), "xl")]
        total = own
        for end in ends:
            total = total + end.astype(jnp.float32)
        outs.append(total * factors[0, low:high, None] * factors[1, low:high, None])
    return (jnp.concatenate(outs, axis=0), token_peak)


def solution(mesh):
    in_specs = (P("col", "row"), P("row"), P("row", "col"))
    out_specs = (P("row", "col"), P("col"))
    return jax.shard_map(shards, mesh=mesh, in_specs=in_specs, out_specs=out_specs, check_vma=False)
```

```python
import jax
import jax.numpy as jnp
from jax import lax
from jax.experimental import pallas as pl
from jax.experimental.pallas import tpu as pltpu
from jax.sharding import PartitionSpec as P

D = 16384
FEATURES = 1024
WIDTH = 3328
AXES = ("row", "col")
TILE = 1664
KEPT = jnp.bfloat16


def place(y, xl, core, z, xh):
    return (y * 4 + xl * 2 + core) * 8 + z * 2 + xh


def pairs(move):
    out = []
    for y in range(4):
        for xl in range(2):
            for core in range(2):
                for z in range(4):
                    for xh in range(2):
                        out.append((place(y, xl, core, z, xh), place(*move(y, xl, core, z, xh))))
    return out


MOVES = {
    "core": pairs(lambda y, xl, core, z, xh: (y, xl, 1 - core, z, xh)),
    "ya": pairs(lambda y, xl, core, z, xh: (y ^ 1, xl, core, z, xh)),
    "yb": pairs(lambda y, xl, core, z, xh: (3 - y, xl, core, z, xh)),
    "xl": pairs(lambda y, xl, core, z, xh: (y, 1 - xl, core, z, xh)),
    "za": pairs(lambda y, xl, core, z, xh: (y, xl, core, z ^ 1, xh)),
    "zb": pairs(lambda y, xl, core, z, xh: (y, xl, core, 3 - z, xh)),
    "xh": pairs(lambda y, xl, core, z, xh: (y, xl, core, z, 1 - xh)),
    "turn": pairs(lambda y, xl, core, z, xh: (z, xh, core, y, xl)),
}


def send(array, move):
    return lax.ppermute(array, AXES, MOVES[move])


def inside(array):
    return pltpu.with_memory_space_constraint(array, pltpu.VMEM)


LOCAL = pl.BlockSpec(memory_space=pltpu.VMEM)


def staged(weight):
    def kernel(source, target, sem):
        copy = pltpu.make_async_copy(source, target, sem)
        copy.start()
        copy.wait()

    return pl.pallas_call(
        kernel,
        in_specs=[pl.BlockSpec(memory_space=pl.ANY)],
        out_specs=LOCAL,
        out_shape=pltpu.VMEM(weight.shape, weight.dtype),
        scratch_shapes=[pltpu.SemaphoreType.DMA(())],
        compiler_params=pltpu.CompilerParams(vmem_limit_bytes=8 << 20),
        cost_estimate=pl.CostEstimate(flops=0, bytes_accessed=14 << 20, transcendentals=0),
        name="staged",
    )(weight)


def multiply(apart, gains, blocks, near, far, totals):
    names = list(blocks)
    rows = blocks[names[0]].shape[1]
    count = len(names) * rows

    def kernel(apart_ref, gain_ref, *refs):
        held, near_ref, far_ref = refs[: len(names)], refs[len(names)], refs[len(names) + 1]
        out, lifted = refs[-2:]
        for side in range(2):
            gain = gain_ref[side : side + 1, :].astype(jnp.float32)
            for n, ref in enumerate(held):
                value = ref[side].astype(jnp.float32) * gain
                lifted[side, n * rows : (n + 1) * rows, :] = value.astype(jnp.bfloat16)
        for low in range(0, WIDTH, TILE):
            where = slice(low, low + TILE)
            got = jnp.dot(lifted[0], near_ref[:, where], preferred_element_type=jnp.float32)
            got += jnp.dot(lifted[1], far_ref[:, where], preferred_element_type=jnp.float32)
            for n, bits in enumerate(names):
                out[apart_ref[0] ^ bits, :, where] = got[n * rows : (n + 1) * rows].astype(out.dtype)

    arrays = [gains] + [inside(blocks[bits]) for bits in names] + [inside(near), inside(far)]
    aliases = {}
    if totals is not None:
        aliases = {len(arrays) + 1: 0}
        arrays.append(inside(totals))
    return pl.pallas_call(
        kernel,
        in_specs=[pl.BlockSpec(memory_space=pltpu.SMEM)] + [LOCAL] * len(arrays),
        out_specs=LOCAL,
        out_shape=pltpu.VMEM((8, rows, WIDTH), KEPT),
        input_output_aliases=aliases,
        scratch_shapes=[pltpu.VMEM((2, count, FEATURES), jnp.bfloat16)],
        compiler_params=pltpu.CompilerParams(vmem_limit_bytes=14 << 20),
        cost_estimate=pl.CostEstimate(flops=4 * count * FEATURES * WIDTH, bytes_accessed=1 << 20, transcendentals=0),
        name="multiply",
    )(apart, *arrays)


def added(totals, index, part, low):
    rows = totals.shape[1]

    def kernel(totals_ref, part_ref, out):
        value = totals_ref[index].astype(jnp.float32)
        if part_ref.shape[0] == rows:
            out[...] = (value + part_ref[...].astype(jnp.float32)).astype(jnp.bfloat16)
        else:
            out[...] = value.astype(jnp.bfloat16)
            here = slice(low, low + part_ref.shape[0])
            out[here, :] = (value[here, :] + part_ref[...].astype(jnp.float32)).astype(jnp.bfloat16)

    return pl.pallas_call(
        kernel,
        in_specs=[LOCAL, LOCAL],
        out_specs=LOCAL,
        out_shape=pltpu.VMEM((rows, WIDTH), jnp.bfloat16),
        compiler_params=pltpu.CompilerParams(vmem_limit_bytes=4 << 20),
        cost_estimate=pl.CostEstimate(flops=rows * WIDTH, bytes_accessed=1 << 10, transcendentals=0),
        name="added",
    )(inside(totals), inside(part))


def sums_away(total):
    half = total.shape[1] // 2
    corner = total[7].astype(jnp.bfloat16)
    to_bx = send(corner[:half], "ya")
    to_ax = send(corner[half:], "yb")
    to_a = send(total[6].astype(jnp.bfloat16), "yb")
    to_b = send(added(total, 3, to_bx, 0), "xl")
    to_x = send(added(total, 5, to_ax, half), "ya")
    ends = (
        send(added(total, 4, to_a, 0), "ya"), send(added(total, 1, to_x, 0), "xl"), send(added(total, 2, to_b, 0), "yb")
    )
    home = total[0].astype(jnp.float32)
    for end in ends:
        home = home + end.astype(jnp.float32)
    return home


def column(own):
    x, b, a = send(own, "xh"), send(own, "zb"), send(own, "za")
    bx, ax, ab = send(x, "zb"), send(x, "za"), send(a, "zb")
    abx = send(bx, "za")
    return {0: own, 4: a, 2: b, 1: x}, {5: ax, 6: ab, 3: bx, 7: abx}


def body(tokens, norm_gain, gate_weight):
    row, col = lax.axis_index("row"), lax.axis_index("col")
    core = row % 2
    y, xl, z, xh = row // 4, (row // 2) % 2, col // 2, col % 2

    def bits(ring, x):
        return (((ring + 1) // 2) % 2) * 4 + (ring // 2) * 2 + x

    apart = (bits(y, xl) ^ bits(z, xh)).reshape(1)
    raw = tokens.reshape(2, 128, FEATURES)
    mine = lax.dynamic_index_in_dim(raw, core, 0)
    theirs = send(lax.dynamic_index_in_dim(raw, 1 - core, 0), "core")
    both = jnp.concatenate([mine, theirs], axis=0)
    far = send(gate_weight, "core")
    near = staged(gate_weight)
    far = staged(far)

    first0, second0 = column(both[:, :64, :])
    first1, second1 = column(both[:, 64:, :])
    norm_gain, tokens, _ = lax.optimization_barrier((norm_gain, tokens, first0[1]))
    gain_row = norm_gain.reshape(1, FEATURES)
    gains = jnp.concatenate([gain_row, send(gain_row, "core")], axis=0)
    total0 = multiply(apart, gains, first0, near, far, None)
    total0 = multiply(apart, gains, second0, near, far, total0)
    total1 = multiply(apart, gains, first1, near, far, None)
    total1 = multiply(apart, gains, second1, near, far, total1)

    values = tokens.astype(jnp.float32)
    squares = jnp.sum(values * values, axis=1)
    peak = jnp.max(jnp.abs(values * norm_gain.astype(jnp.float32)[None, :]), axis=1)
    stats = jnp.stack([squares, peak])
    for move in ("core", "ya", "yb", "xl"):
        other = send(stats, move)
        stats = jnp.stack([stats[0] + other[0], jnp.maximum(stats[1], other[1])])
    inverse = lax.rsqrt(stats[0] / D + 1e-05)
    token_peak = stats[1] * inverse
    scale = ((token_peak + 1e-06) / 448.0).astype(jnp.bfloat16).astype(jnp.float32)
    factors = jnp.stack([inverse / scale, scale]).reshape(2, 2, 128)
    factors = send(lax.dynamic_index_in_dim(factors, core, 1, keepdims=False), "turn")

    home = jnp.concatenate([sums_away(total0), sums_away(total1)], axis=0)
    return (home * factors[0, :, None] * factors[1, :, None], token_peak)


def solution(mesh):
    in_specs = (P("col", "row"), P("row"), P("row", "col"))
    out_specs = (P("row", "col"), P("col"))
    return jax.shard_map(body, mesh=mesh, in_specs=in_specs, out_specs=out_specs, check_vma=False)
```

```python
import jax
import jax.numpy as jnp
from jax import lax
from jax.experimental import pallas as pl
from jax.experimental.pallas import tpu as pltpu
from jax.sharding import PartitionSpec as P

D = 16384
FEATURES = 1024
WIDTH = 3328
AXES = ("row", "col")
TILE = 1664
KEPT = jnp.bfloat16


def place(y, xl, core, z, xh):
    return (y * 4 + xl * 2 + core) * 8 + z * 2 + xh


def pairs(move):
    out = []
    for y in range(4):
        for xl in range(2):
            for core in range(2):
                for z in range(4):
                    for xh in range(2):
                        out.append((place(y, xl, core, z, xh), place(*move(y, xl, core, z, xh))))
    return out


MOVES = {
    "core": pairs(lambda y, xl, core, z, xh: (y, xl, 1 - core, z, xh)),
    "ya": pairs(lambda y, xl, core, z, xh: (y ^ 1, xl, core, z, xh)),
    "yb": pairs(lambda y, xl, core, z, xh: (3 - y, xl, core, z, xh)),
    "xl": pairs(lambda y, xl, core, z, xh: (y, 1 - xl, core, z, xh)),
    "za": pairs(lambda y, xl, core, z, xh: (y, xl, core, z ^ 1, xh)),
    "zb": pairs(lambda y, xl, core, z, xh: (y, xl, core, 3 - z, xh)),
    "xh": pairs(lambda y, xl, core, z, xh: (y, xl, core, z, 1 - xh)),
    "turn": pairs(lambda y, xl, core, z, xh: (z, xh, core, y, xl)),
}


def send(array, move):
    return lax.ppermute(array, AXES, MOVES[move])


def inside(array):
    return pltpu.with_memory_space_constraint(array, pltpu.VMEM)


LOCAL = pl.BlockSpec(memory_space=pltpu.VMEM)


def staged(weight):
    def kernel(source, target, sem):
        copy = pltpu.make_async_copy(source, target, sem)
        copy.start()
        copy.wait()

    return pl.pallas_call(
        kernel,
        in_specs=[pl.BlockSpec(memory_space=pl.ANY)],
        out_specs=LOCAL,
        out_shape=pltpu.VMEM(weight.shape, weight.dtype),
        scratch_shapes=[pltpu.SemaphoreType.DMA(())],
        compiler_params=pltpu.CompilerParams(vmem_limit_bytes=1 << 20),
        cost_estimate=pl.CostEstimate(flops=0, bytes_accessed=14 << 20, transcendentals=0),
        name="staged",
    )(weight)


def multiply(apart, gains, blocks, near, far, totals):
    names = list(blocks)
    rows = blocks[names[0]].shape[1]
    count = len(names) * rows

    def kernel(apart_ref, gain_ref, *refs):
        held, near_ref, far_ref = refs[: len(names)], refs[len(names)], refs[len(names) + 1]
        out, lifted = refs[-2:]
        for side in range(2):
            gain = gain_ref[side : side + 1, :].astype(jnp.float32)
            for n, ref in enumerate(held):
                value = ref[side].astype(jnp.float32) * gain
                lifted[side, n * rows : (n + 1) * rows, :] = value.astype(jnp.bfloat16)
        for low in range(0, WIDTH, TILE):
            where = slice(low, low + TILE)
            got = jnp.dot(lifted[0], near_ref[:, where], preferred_element_type=jnp.float32)
            got += jnp.dot(lifted[1], far_ref[:, where], preferred_element_type=jnp.float32)
            for n, bits in enumerate(names):
                out[apart_ref[0] ^ bits, :, where] = got[n * rows : (n + 1) * rows].astype(out.dtype)

    arrays = [gains] + [inside(blocks[bits]) for bits in names] + [inside(near), inside(far)]
    aliases = {}
    if totals is not None:
        aliases = {len(arrays) + 1: 0}
        arrays.append(inside(totals))
    return pl.pallas_call(
        kernel,
        in_specs=[pl.BlockSpec(memory_space=pltpu.SMEM)] + [LOCAL] * len(arrays),
        out_specs=LOCAL,
        out_shape=pltpu.VMEM((8, rows, WIDTH), KEPT),
        input_output_aliases=aliases,
        scratch_shapes=[pltpu.VMEM((2, count, FEATURES), jnp.bfloat16)],
        compiler_params=pltpu.CompilerParams(vmem_limit_bytes=6 << 20),
        cost_estimate=pl.CostEstimate(flops=4 * count * FEATURES * WIDTH, bytes_accessed=1 << 20, transcendentals=0),
        name="multiply",
    )(apart, *arrays)


def multiply_first(apart, gains, blocks, near, far):
    names = list(blocks)
    rows = blocks[names[0]].shape[1]
    count = len(names) * rows

    def kernel(apart_ref, gain_ref, *refs):
        held, near_ref, source = refs[: len(names)], refs[len(names)], refs[len(names) + 1]
        out, far_ref, lifted, part, sem = refs[-5:]
        copy = pltpu.make_async_copy(source, far_ref, sem)
        copy.start()
        for side in range(2):
            gain = gain_ref[side : side + 1, :].astype(jnp.float32)
            for n, ref in enumerate(held):
                value = ref[side].astype(jnp.float32) * gain
                lifted[side, n * rows : (n + 1) * rows, :] = value.astype(jnp.bfloat16)
        for low in range(0, WIDTH, TILE):
            where = slice(low, low + TILE)
            part[:, where] = jnp.dot(lifted[0], near_ref[:, where], preferred_element_type=jnp.float32)
        copy.wait()
        for low in range(0, WIDTH, TILE):
            where = slice(low, low + TILE)
            got = jnp.dot(lifted[1], far_ref[:, where], preferred_element_type=jnp.float32)
            got += part[:, where]
            for n, bits in enumerate(names):
                out[apart_ref[0] ^ bits, :, where] = got[n * rows : (n + 1) * rows].astype(out.dtype)

    arrays = [gains] + [inside(blocks[bits]) for bits in names] + [inside(near)]
    return pl.pallas_call(
        kernel,
        in_specs=[pl.BlockSpec(memory_space=pltpu.SMEM)]
        + [LOCAL] * len(arrays)
        + [pl.BlockSpec(memory_space=pl.ANY)],
        out_specs=[LOCAL, LOCAL],
        out_shape=[pltpu.VMEM((8, rows, WIDTH), KEPT), pltpu.VMEM(far.shape, far.dtype)],
        scratch_shapes=[
            pltpu.VMEM((2, count, FEATURES), jnp.bfloat16),
            pltpu.VMEM((count, WIDTH), jnp.float32),
            pltpu.SemaphoreType.DMA(()),
        ],
        compiler_params=pltpu.CompilerParams(vmem_limit_bytes=10 << 20),
        cost_estimate=pl.CostEstimate(flops=4 * count * FEATURES * WIDTH, bytes_accessed=8 << 20, transcendentals=0),
        name="multiply_first",
    )(apart, *arrays, far)


def added(totals, index, part, low):
    rows = totals.shape[1]

    def kernel(totals_ref, part_ref, out):
        value = totals_ref[index].astype(jnp.float32)
        if part_ref.shape[0] == rows:
            out[...] = (value + part_ref[...].astype(jnp.float32)).astype(jnp.bfloat16)
        else:
            out[...] = value.astype(jnp.bfloat16)
            here = slice(low, low + part_ref.shape[0])
            out[here, :] = (value[here, :] + part_ref[...].astype(jnp.float32)).astype(jnp.bfloat16)

    return pl.pallas_call(
        kernel,
        in_specs=[LOCAL, LOCAL],
        out_specs=LOCAL,
        out_shape=pltpu.VMEM((rows, WIDTH), jnp.bfloat16),
        compiler_params=pltpu.CompilerParams(vmem_limit_bytes=2 << 20),
        cost_estimate=pl.CostEstimate(flops=rows * WIDTH, bytes_accessed=1 << 10, transcendentals=0),
        name="added",
    )(inside(totals), inside(part))


def sums_away(total):
    half = total.shape[1] // 2
    corner = total[7].astype(jnp.bfloat16)
    to_bx = send(corner[:half], "ya")
    to_ax = send(corner[half:], "yb")
    to_a = send(total[6].astype(jnp.bfloat16), "yb")
    to_b = send(added(total, 3, to_bx, 0), "xl")
    to_x = send(added(total, 5, to_ax, half), "ya")
    ends = (
        send(added(total, 4, to_a, 0), "ya"), send(added(total, 1, to_x, 0), "xl"), send(added(total, 2, to_b, 0), "yb")
    )
    home = total[0].astype(jnp.float32)
    for end in ends:
        home = home + end.astype(jnp.float32)
    return home


def column(own):
    x, b, a = send(own, "xh"), send(own, "zb"), send(own, "za")
    bx, ax, ab = send(x, "zb"), send(x, "za"), send(a, "zb")
    abx = send(bx, "za")
    return {0: own, 4: a, 2: b, 1: x}, {5: ax, 6: ab, 3: bx, 7: abx}


def body(tokens, norm_gain, gate_weight):
    row, col = lax.axis_index("row"), lax.axis_index("col")
    core = row % 2
    y, xl, z, xh = row // 4, (row // 2) % 2, col // 2, col % 2

    def bits(ring, x):
        return (((ring + 1) // 2) % 2) * 4 + (ring // 2) * 2 + x

    apart = (bits(y, xl) ^ bits(z, xh)).reshape(1)
    raw = tokens.reshape(2, 128, FEATURES)
    mine = lax.dynamic_index_in_dim(raw, core, 0)
    gain_rows = jnp.broadcast_to(norm_gain[None, None, :], (1, 16, FEATURES))
    leaving = jnp.concatenate([lax.dynamic_index_in_dim(raw, 1 - core, 0), gain_rows], axis=1)
    theirs = send(leaving, "core")
    far = send(gate_weight, "core")
    near = staged(gate_weight)

    both = jnp.concatenate([mine, theirs[:, :128, :]], axis=0)
    first0, second0 = column(both[:, :64, :])
    first1, second1 = column(both[:, 64:, :])
    leaving, theirs, both, _ = lax.optimization_barrier((leaving, theirs, both, first0[1]))
    gains = jnp.concatenate([leaving[0, 128:129, :], theirs[0, 128:129, :]], axis=0)
    total0, far = multiply_first(apart, gains, first0, near, far)
    total0 = multiply(apart, gains, second0, near, far, total0)
    total1 = multiply(apart, gains, first1, near, far, None)
    total1 = multiply(apart, gains, second1, near, far, total1)

    values = both.astype(jnp.float32)
    squares = jnp.sum(values * values, axis=(0, 2))
    peak = jnp.max(jnp.abs(values * gains.astype(jnp.float32)[:, None, :]), axis=(0, 2))
    stats = jnp.stack([squares, peak])
    for move in ("ya", "yb", "xl"):
        other = send(stats, move)
        stats = jnp.stack([stats[0] + other[0], jnp.maximum(stats[1], other[1])])
    inverse = lax.rsqrt(stats[0] / D + 1e-05)
    peak_here = stats[1] * inverse
    scale = lax.reduce_precision((peak_here + 1e-06) / 448.0, 8, 7)
    factors = send(jnp.stack([inverse / scale, scale]), "turn")
    peak_there = send(peak_here, "core")
    peaks = jnp.stack([peak_here, peak_there])
    token_peak = jnp.concatenate(
        [lax.dynamic_index_in_dim(peaks, core, 0, False), lax.dynamic_index_in_dim(peaks, 1 - core, 0, False)]
    )

    home = jnp.concatenate([sums_away(total0), sums_away(total1)], axis=0)
    return (home * factors[0, :, None] * factors[1, :, None], token_peak)


def solution(mesh):
    in_specs = (P("col", "row"), P("row"), P("row", "col"))
    out_specs = (P("row", "col"), P("col"))
    return jax.shard_map(body, mesh=mesh, in_specs=in_specs, out_specs=out_specs, check_vma=False)
```
